32 devices in a mesh: wide: 8 (over y, x, core), narrow: 4 (over z).
Axes of the slice: x: 2, y: 2, z: 4, core: 2. Of those that a mesh axis runs over, the one named last changes fastest.
Arguments:
- query_tokens: bfloat16 [128, 32, 768], P(('wide', 'narrow')), may hold values from -6 to 6
- query_mask: int32 [128, 32], P(('wide', 'narrow')), may hold values from 0 to 1, as said below
- short_tokens: bfloat16 [32, 64, 768], P(('wide', 'narrow')), may hold values from -6 to 6
- short_mask: int32 [32, 64], P(('wide', 'narrow')), may hold values from 0 to 1, as said below
- long_tokens: bfloat16 [64, 256, 768], P(('wide', 'narrow')), may hold values from -6 to 6
- long_mask: int32 [64, 256], P(('wide', 'narrow')), may hold values from 0 to 1, as said below
- long_count: int32 [32], P(('wide', 'narrow')), may hold values from 1 to 2, as said below
- query_inproj: bfloat16 [768, 2304], P('wide'), may hold values from -0.21875 to 0.21875
- query_outproj: bfloat16 [768, 768], P('wide'), may hold values from -0.625 to 0.625
- query_ffn_up: bfloat16 [768, 3072], P('wide'), may hold values from -0.21875 to 0.21875
- query_ffn_down: bfloat16 [3072, 768], P('wide'), may hold values from -0.109375 to 0.109375
- query_gains: float32 [2, 768], P(None, 'wide'), may hold values from 0.5 to 1.5
- query_biases: float32 [6, 768], P(None, 'wide'), may hold values from -3 to 3
- query_up_bias: float32 [3072], P('wide'), may hold values from -3 to 3
- passage_inproj: bfloat16 [768, 2304], P('wide'), may hold values from -0.21875 to 0.21875
- passage_outproj: bfloat16 [768, 768], P('wide'), may hold values from -0.625 to 0.625
- passage_ffn_up: bfloat16 [768, 3072], P('wide'), may hold values from -0.21875 to 0.21875
- passage_ffn_down: bfloat16 [3072, 768], P('wide'), may hold values from -0.109375 to 0.109375
- passage_gains: float32 [2, 768], P(None, 'wide'), may hold values from 0.5 to 1.5
- passage_biases: float32 [6, 768], P(None, 'wide'), may hold values from -3 to 3
- passage_up_bias: float32 [3072], P('wide'), may hold values from -3 to 3
- query_upstream: bfloat16 [128, 32, 768], P(('wide', 'narrow')), may hold values from -6 to 6
- short_upstream: bfloat16 [32, 64, 768], P(('wide', 'narrow')), may hold values from -6 to 6
- long_upstream: bfloat16 [64, 256, 768], P(('wide', 'narrow')), may hold values from -6 to 6
Outputs:
- query_output: bfloat16 [128, 32, 768], P(('wide', 'narrow'))
- short_output: bfloat16 [32, 64, 768], P(('wide', 'narrow'))
- long_output: bfloat16 [64, 256, 768], P(('wide', 'narrow'))
- query_tokens_gradient: float32 [128, 32, 768], P(('wide', 'narrow'))
- short_tokens_gradient: float32 [32, 64, 768], P(('wide', 'narrow'))
- long_tokens_gradient: float32 [64, 256, 768], P(('wide', 'narrow'))
- query_inproj_gradient: float32 [768, 2304], P('wide')
- query_outproj_gradient: float32 [768, 768], P('wide')
- query_ffn_up_gradient: float32 [768, 3072], P('wide')
- query_ffn_down_gradient: float32 [3072, 768], P('wide')
- query_gains_gradient: float32 [2, 768], P(None, 'wide')
- query_biases_gradient: float32 [6, 768], P(None, 'wide')
- query_up_bias_gradient: float32 [3072], P('wide')
- passage_inproj_gradient: float32 [768, 2304], P('wide')
- passage_outproj_gradient: float32 [768, 768], P('wide')
- passage_ffn_up_gradient: float32 [768, 3072], P('wide')
- passage_ffn_down_gradient: float32 [3072, 768], P('wide')
- passage_gains_gradient: float32 [2, 768], P(None, 'wide')
- passage_biases_gradient: float32 [6, 768], P(None, 'wide')
- passage_up_bias_gradient: float32 [3072], P('wide')
The draws below stay inside these ranges and needn't reach their ends.
Inputs may be any that keep to these rules, and one draw needn't show every extreme that they name: `query_mask`: the ones of each row form a prefix of 8 to 32 positions; row 0 is all ones. `short_mask`: the ones of each row form a prefix of 16 to 64 positions; row 0 is all ones. `long_mask`: the ones of each row form a prefix of 64 to 256 positions; row 0 is all ones. `long_count`: entry i counts the live long passages among the 2 slots of the i-th block of rows; the first ones are live, the rest are empty. Some device has all 2 live and some has one.
All inputs are finite; a program needn't handle non-finite values.
Results may differ from the reference program's by a relative error of at most 0.024.
Values may be sent and summed in bfloat16 or wider, within the bound.
No kernel may reach another device: no remote copies, remote signals or barrier semaphores. Data moves between devices by JAX's collectives and lax.ppermute only.
A program may use at most 120 MiB of HBM per device.

```python
import math
import jax
import jax.numpy as jnp
from jax import lax

D = 768
HEADS = 12
FF = 3072
QLEN = 32
SLEN = 64
LLEN = 256
LONG_DEV = 2
QROWS = 128
SROWS = 32
LROWS = 64
DEVICES = 32


def prefix_mask(key, row_count, length):
    filled = jax.random.randint(key, (row_count,), length // 4, length + 1)
    filled = filled.at[0].set(length)
    return (jnp.arange(length)[None, :] < filled[:, None]).astype(jnp.int32)


def draw_query_mask(key, part):
    return prefix_mask(key, QROWS, QLEN)


def draw_short_mask(key, part):
    return prefix_mask(key, SROWS, SLEN)


def draw_long_mask(key, part):
    return prefix_mask(key, LROWS, LLEN)


def draw_long_count(key, part):
    counts = jax.random.randint(key, (DEVICES,), 1, LONG_DEV + 1)
    return counts.at[0].set(LONG_DEV).at[1].set(1).astype(jnp.int32)


def levels(key, shape, pieces, smallest, largest):
    loudness = 1.0
    for axis_at, shards_of in pieces:
        heights = jax.random.uniform(jax.random.fold_in(jax.random.fold_in(key, 6), axis_at), (shards_of,), jnp.float32, smallest / len(pieces), largest / len(pieces))
        loudness = loudness * jnp.repeat(jnp.exp(heights), shape[axis_at] // shards_of).reshape((-1,) + (1,) * (len(shape) - 1 - axis_at))
    return loudness


def normal_values(rng, shape, scale, most, pieces=(), kind=jnp.bfloat16):
    values = scale * jax.random.normal(rng, shape, jnp.float32)
    if pieces:
        values = values * levels(rng, shape, pieces, -0.22, 0.18)
    return jnp.clip(values, -most, most).astype(kind)


def setup_inputs(seed: int = 0) -> dict:
    streams_of = jax.random.split(jax.random.key(seed), 25)
    return {
        "query_tokens": normal_values(streams_of[0], (QROWS, QLEN, D), 1.0, 6.0, ((0, 32),)),
        "query_mask": draw_query_mask(jax.random.fold_in(streams_of[24], 71), 0),
        "short_tokens": normal_values(streams_of[2], (SROWS, SLEN, D), 1.0, 6.0, ((0, 32),)),
        "short_mask": draw_short_mask(jax.random.fold_in(streams_of[24], 71), 0),
        "long_tokens": normal_values(streams_of[4], (LROWS, LLEN, D), 1.0, 6.0, ((0, 32),)),
        "long_mask": draw_long_mask(jax.random.fold_in(streams_of[24], 71), 0),
        "long_count": draw_long_count(jax.random.fold_in(streams_of[24], 71), 0),
        "query_inproj": normal_values(streams_of[7], (D, 3 * D), D ** -0.5, 0.21875, ((0, 8),)),
        "query_outproj": normal_values(streams_of[8], (D, D), (D // 8) ** -0.5, 0.625, ((0, 8),)),
        "query_ffn_up": normal_values(streams_of[9], (D, FF), D ** -0.5, 0.21875, ((0, 8),)),
        "query_ffn_down": normal_values(streams_of[10], (FF, D), FF ** -0.5, 0.109375, ((0, 8),)),
        "query_gains": jnp.clip(1.0 + 0.1 * jax.random.normal(streams_of[11], (2, D), jnp.float32), 0.5, 1.5),
        "query_biases": normal_values(streams_of[12], (6, D), 0.5, 3.0, ((1, 8),), jnp.float32),
        "query_up_bias": normal_values(streams_of[13], (FF,), 0.5, 3.0, ((0, 8),), jnp.float32),
        "passage_inproj": normal_values(streams_of[14], (D, 3 * D), D ** -0.5, 0.21875, ((0, 8),)),
        "passage_outproj": normal_values(streams_of[15], (D, D), (D // 8) ** -0.5, 0.625, ((0, 8),)),
        "passage_ffn_up": normal_values(streams_of[16], (D, FF), D ** -0.5, 0.21875, ((0, 8),)),
        "passage_ffn_down": normal_values(streams_of[17], (FF, D), FF ** -0.5, 0.109375, ((0, 8),)),
        "passage_gains": jnp.clip(1.0 + 0.1 * jax.random.normal(streams_of[18], (2, D), jnp.float32), 0.5, 1.5),
        "passage_biases": normal_values(streams_of[19], (6, D), 0.5, 3.0, ((1, 8),), jnp.float32),
        "passage_up_bias": normal_values(streams_of[20], (FF,), 0.5, 3.0, ((0, 8),), jnp.float32),
        "query_upstream": normal_values(streams_of[21], (QROWS, QLEN, D), 1.0, 6.0, ((0, 32),)),
        "short_upstream": normal_values(streams_of[22], (SROWS, SLEN, D), 1.0, 6.0, ((0, 32),)),
        "long_upstream": normal_values(streams_of[23], (LROWS, LLEN, D), 1.0, 6.0, ((0, 32),)),
    }


@jax.custom_vjp
def low(v):
    return lax.optimization_barrier(v.astype(jnp.bfloat16)).astype(jnp.float32)

@jax.custom_vjp
def low_back(v):
    return v

def low_keep(v):
    return (low(v), None)

def low_pass(kept, grad):
    return (grad,)

def back_keep(v):
    return (v, None)

def back_low(kept, grad):
    return (low(grad),)
low.defvjp(low_keep, low_pass)
low_back.defvjp(back_keep, back_low)
EPSILON = 1e-05
NEGATIVE = -1000000000.0
ROOT_HALF = 0.7071067811865476

def product(left, right):
    return jnp.matmul(left, right, precision=lax.Precision.HIGHEST)

def layer_norm(hidden, gain, shift):
    center = hidden - lax.optimization_barrier(jnp.mean(hidden, axis=-1, keepdims=True))
    variance = lax.optimization_barrier(jnp.mean(center * center, axis=-1, keepdims=True))
    return center * lax.rsqrt(variance + EPSILON) * gain + shift

def gelu_exact(values):
    return 0.5 * values * (1.0 + lax.erf(values * ROOT_HALF))

def tower_layer(params, tokens, alive_mask):
    inproj, outproj, ffn_up, ffn_down, gain_rows, biases, up_bias = params
    row_count, length, features = tokens.shape
    head_size = features // HEADS
    layout = (row_count, length, HEADS, head_size)
    joined = product(tokens, inproj)
    queries = low(low_back(joined[..., :features] + biases[0])).reshape(layout)
    key_rows = low(low_back(joined[..., features:2 * features])).reshape(layout)
    values = low(low_back(joined[..., 2 * features:] + biases[1])).reshape(layout)
    scores = jnp.einsum('bqhe,bkhe->bhqk', queries, key_rows, precision=lax.Precision.HIGHEST) * head_size ** (-0.5)
    scores = low_back(scores)
    visible = (alive_mask > 0)[:, None, None, :]
    masked = jnp.where(visible, scores, NEGATIVE)
    highest = lax.optimization_barrier(jnp.max(masked, axis=-1, keepdims=True))
    exponent = jnp.exp(masked - highest)
    probs = low(exponent / lax.optimization_barrier(jnp.sum(exponent, axis=-1, keepdims=True)))
    blended = jnp.einsum('bhqk,bkhe->bqhe', probs, values, precision=lax.Precision.HIGHEST)
    blended = low(low_back(blended.reshape(row_count, length, features)))
    branch = low_back(product(blended, outproj) + biases[2])
    first_out = layer_norm(tokens + branch, gain_rows[0], biases[3])
    expanded = low_back(product(low(first_out), ffn_up) + up_bias)
    activated = low(gelu_exact(expanded))
    second = low_back(product(activated, ffn_down) + biases[4])
    return layer_norm(first_out + second, gain_rows[1], biases[5])

def bucket_pass(params, tokens, mask, upstream, alive_rows):
    row_count, length, features = tokens.shape
    per_block = math.gcd(row_count, max(1, 4096 // length))
    blocks = row_count // per_block
    live = mask * alive_rows[:, None]

    def shaped(array):
        return array.reshape((blocks, per_block) + array.shape[1:])
    initial = jax.tree.map(jnp.zeros_like, params)

    def advance(summed, segment):
        block_tokens, block_live, block_upstream = segment

        def forward(weights, inputs):
            return tower_layer(weights, inputs, block_live)
        outputs, pullback = jax.vjp(forward, params, block_tokens.astype(jnp.float32))
        weighting = (block_live > 0).astype(jnp.float32)[..., None]
        weight_grads, input_grads = pullback(block_upstream.astype(jnp.float32) * weighting)
        summed = jax.tree.map(jnp.add, summed, weight_grads)
        return (summed, (outputs.astype(jnp.bfloat16), input_grads))
    summed, (outputs, input_grads) = lax.scan(advance, initial, (shaped(tokens), shaped(live), shaped(upstream)))
    return (summed, outputs.reshape(tokens.shape), input_grads.reshape(tokens.shape))

def reference(query_tokens, query_mask, short_tokens, short_mask, long_tokens, long_mask, long_count, query_inproj, query_outproj, query_ffn_up, query_ffn_down, query_gains, query_biases, query_up_bias, passage_inproj, passage_outproj, passage_ffn_up, passage_ffn_down, passage_gains, passage_biases, passage_up_bias, query_upstream, short_upstream, long_upstream):
    query_params = tuple((weight.astype(jnp.float32) for weight in (query_inproj, query_outproj, query_ffn_up, query_ffn_down, query_gains, query_biases, query_up_bias)))
    passage_params = tuple((weight.astype(jnp.float32) for weight in (passage_inproj, passage_outproj, passage_ffn_up, passage_ffn_down, passage_gains, passage_biases, passage_up_bias)))
    query_alive = jnp.ones((query_tokens.shape[0],), jnp.int32)
    short_alive = jnp.ones((short_tokens.shape[0],), jnp.int32)
    slot_index = jnp.arange(long_tokens.shape[0], dtype=jnp.int32) % LONG_DEV
    long_alive = (slot_index < jnp.repeat(long_count, LONG_DEV, total_repeat_length=long_tokens.shape[0])).astype(jnp.int32)
    query_grads, query_output, query_gradient = bucket_pass(query_params, query_tokens, query_mask, query_upstream, query_alive)
    short_grads, short_output, short_gradient = bucket_pass(passage_params, short_tokens, short_mask, short_upstream, short_alive)
    long_grads, long_output, long_gradient = bucket_pass(passage_params, long_tokens, long_mask, long_upstream, long_alive)
    passage_grads = jax.tree.map(jnp.add, short_grads, long_grads)
    return (query_output, short_output, long_output, query_gradient, short_gradient, long_gradient, query_grads[0], query_grads[1], query_grads[2], query_grads[3], query_grads[4], query_grads[5], query_grads[6], passage_grads[0], passage_grads[1], passage_grads[2], passage_grads[3], passage_grads[4], passage_grads[5], passage_grads[6])
```

```python
import functools

import jax
import jax.numpy as jnp
from jax import lax
from jax.experimental import pallas as pl
from jax.experimental.pallas import tpu as pltpu
from jax.sharding import PartitionSpec as P

HEADS = 12


EPSILON = 1e-05
NEGATIVE = -1000000000.0
ROOT_HALF = 0.7071067811865476
INV_ROOT_TAU = 0.3989422804014327


def matmul(left, right):
    return jnp.dot(left, right, preferred_element_type=jnp.float32)


def contract_rows(left, right):
    return lax.dot_general(
        left, right, (((0,), (0,)), ((), ())), preferred_element_type=jnp.float32
    )


def times_transposed(left, right):
    return lax.dot_general(
        left, right, (((1,), (1,)), ((), ())), preferred_element_type=jnp.float32
    )


def normalize(hidden):
    center = hidden - jnp.mean(hidden, axis=-1, keepdims=True)
    scaling = lax.rsqrt(jnp.mean(center * center, axis=-1, keepdims=True) + EPSILON)
    return (center * scaling, scaling)


def norm_back(upstream, normed, scaling, gain):
    scaled = upstream * gain
    return scaling * (
        scaled
        - jnp.mean(scaled, axis=-1, keepdims=True)
        - normed * jnp.mean(scaled * normed, axis=-1, keepdims=True)
    )


def gelu_exact(values):
    return 0.5 * values * (1.0 + lax.erf(values * ROOT_HALF))


def gelu_slope(values):
    return (
        0.5 * (1.0 + lax.erf(values * ROOT_HALF))
        + values * jnp.exp(-0.5 * values * values) * INV_ROOT_TAU
    )


def bucket_rows(array, offset, row_count, length):
    return array[offset : offset + row_count * length].reshape(row_count, length, array.shape[-1])


def split_heads(array):
    row_count, length, features = array.shape
    return array.reshape(row_count, length, HEADS, features // HEADS)


def masked_scores(queries, key_rows, alive_mask):
    head_size = queries.shape[-1] // HEADS
    scores = jnp.einsum(
        "bqhe,bkhe->bhqk",
        split_heads(queries),
        split_heads(key_rows),
        preferred_element_type=jnp.float32,
    ) * head_size ** (-0.5)
    visible = (alive_mask > 0)[:, None, None, :]
    return (jnp.where(visible, scores, NEGATIVE), head_size ** (-0.5))


def attend(queries, key_rows, values, alive_mask):
    masked, factor = masked_scores(queries, key_rows, alive_mask)
    highest = jnp.max(masked, axis=-1, keepdims=True)
    exponent = jnp.exp(masked - highest)
    totals = jnp.sum(exponent, axis=-1, keepdims=True)
    weights = (exponent / totals).astype(jnp.bfloat16)
    blended = jnp.einsum(
        "bhqk,bkhe->bqhe", weights, split_heads(values), preferred_element_type=jnp.float32
    )
    return (blended.astype(jnp.bfloat16), highest + jnp.log(totals))


def attend_back(queries, key_rows, values, alive_mask, logsum, upstream):
    row_count, length, features = queries.shape
    masked, factor = masked_scores(queries, key_rows, alive_mask)
    probs = jnp.exp(masked - logsum)
    weights = probs.astype(jnp.bfloat16)
    upstream_heads = split_heads(upstream)
    value_grad = jnp.einsum(
        "bhqk,bqhe->bkhe", weights, upstream_heads, preferred_element_type=jnp.float32
    ).astype(jnp.bfloat16)
    prob_grad = jnp.einsum(
        "bqhe,bkhe->bhqk", upstream_heads, split_heads(values), preferred_element_type=jnp.float32
    )
    intersection = jnp.sum(probs * prob_grad, axis=-1, keepdims=True)
    score_grad = (probs * (prob_grad - intersection)).astype(jnp.bfloat16)
    query_grad = (
        jnp.einsum(
            "bhqk,bkhe->bqhe", score_grad, split_heads(key_rows), preferred_element_type=jnp.float32
        )
        * factor
    ).astype(jnp.bfloat16)
    key_grad = (
        jnp.einsum(
            "bhqk,bqhe->bkhe", score_grad, split_heads(queries), preferred_element_type=jnp.float32
        )
        * factor
    ).astype(jnp.bfloat16)
    flat_rows = row_count * length
    return jnp.concatenate(
        [
            query_grad.reshape(flat_rows, features),
            key_grad.reshape(flat_rows, features),
            value_grad.reshape(flat_rows, features),
        ],
        axis=1,
    )


def add_low(left, right):
    return (left.astype(jnp.float32) + right.astype(jnp.float32)).astype(jnp.bfloat16)


class Links:
    def __init__(self, mesh):
        self.wide = mesh.shape["wide"]
        self.narrow = mesh.shape["narrow"]
        levels = self.wide.bit_length() - 1
        upward = list(range(1, levels))
        self.orders = (upward, upward[1:] + upward[:1])
        self.steps = [
            [(w, w ^ (1 << self.orders[w & 1][s])) for w in range(self.wide)]
            for s in range(levels - 1)
        ]
        self.swap = [(w, w ^ 1) for w in range(self.wide)]

    def place(self):
        spot = lax.axis_index("wide").astype(jnp.int32)
        return (spot, spot & 1)

    def shifts(self, core):
        return [
            jnp.where(core == 0, first, second).astype(jnp.int32)
            for first, second in zip(*self.orders)
        ]

    def targets(self, slots):
        spot, core = self.place()
        half = self.wide // 2
        away = slots >= half
        inner = jnp.where(away, slots - half, slots)
        masks = jnp.where(away, 1, 0)
        for s, (mine, other) in enumerate(zip(self.shifts(core), self.shifts(1 - core))):
            bit = (inner >> s) & 1
            masks = masks | jnp.where(away, bit << other, bit << mine)
        return spot ^ masks

    def slots_of_chips(self):
        spot, core = self.place()
        chip_mask = jnp.arange(self.wide // 2, dtype=jnp.int32) ^ (spot >> 1)
        found = []
        for shifts in (self.shifts(core), self.shifts(1 - core)):
            slot = jnp.zeros_like(chip_mask)
            for s, shift in enumerate(shifts):
                slot = slot | (((chip_mask >> (shift - 1)) & 1) << s)
            found.append(slot)
        return found, core

    def gather(self, shard):
        held = shard[None]
        for step in self.steps:
            held = jnp.concatenate([held, lax.ppermute(held, "wide", step)], axis=0)
        return held, lax.ppermute(held, "wide", self.swap)

    def scatter(self, summed):
        for step in reversed(self.steps):
            half = summed.shape[0] // 2
            summed = add_low(summed[:half], lax.ppermute(summed[half:], "wide", step))
        return summed[0]

    def narrow_sum(self, terms):
        count = self.narrow
        rows = terms.shape[0]
        if count & (count - 1) or rows % count:
            return lax.psum(terms, "narrow")
        spot = lax.axis_index("narrow")
        strides = []
        stride = 1
        while stride < count:
            swap = [(z, z ^ stride) for z in range(count)]
            half = terms.shape[0] // 2
            low_side = (spot & stride) == 0
            kept = jnp.where(low_side, terms[:half], terms[half:])
            sent = jnp.where(low_side, terms[half:], terms[:half])
            terms = lax.optimization_barrier(add_low(kept, lax.ppermute(sent, "narrow", swap)))
            strides.append((swap, low_side))
            stride *= 2
        for swap, low_side in reversed(strides):
            other = lax.ppermute(terms, "narrow", swap)
            terms = jnp.where(
                low_side,
                jnp.concatenate([terms, other], axis=0),
                jnp.concatenate([other, terms], axis=0),
            )
        return terms


def settle(links, held, partner, widths):
    (own_slots, partner_slots), core = links.slots_of_chips()
    chips, rows, columns = held.shape
    bounds = [0]
    for width in widths:
        bounds.append(bounds[-1] + width)

    def body(own_ref, partner_ref, core_ref, held_ref, other_ref, *outs):
        for flag, first, second in ((0, held_ref, other_ref), (1, other_ref, held_ref)):

            @pl.when(core_ref[0] == flag)
            def _():
                for at, out in enumerate(outs):
                    out[0, 0] = first[0, :, bounds[at] : bounds[at + 1]]
                    out[0, 1] = second[0, :, bounds[at] : bounds[at + 1]]

    outs = pl.pallas_call(
        body,
        grid_spec=pltpu.PrefetchScalarGridSpec(
            num_scalar_prefetch=3,
            grid=(chips,),
            in_specs=[
                pl.BlockSpec((1, rows, columns), lambda q, own, partner, core: (own[q], 0, 0)),
                pl.BlockSpec((1, rows, columns), lambda q, own, partner, core: (partner[q], 0, 0)),
            ],
            out_specs=[
                pl.BlockSpec((1, 2, rows, width), lambda q, own, partner, core: (q, 0, 0, 0))
                for width in widths
            ],
        ),
        out_shape=[jax.ShapeDtypeStruct((chips, 2, rows, width), held.dtype) for width in widths],
        cost_estimate=pl.CostEstimate(
            flops=0, bytes_accessed=8 * held.size, transcendentals=0
        ),
        name="settle",
    )(own_slots, partner_slots, core[None], held, partner)
    return [out.reshape(-1, out.shape[-1]) for out in outs]


def fetch(links, shards):
    inproj_part, outproj_part, up_part, down_part = shards
    front = jnp.concatenate([inproj_part, outproj_part], axis=1)
    inproj, outproj = settle(
        links, *links.gather(front), (inproj_part.shape[1], outproj_part.shape[1])
    )
    (ffn_up,) = settle(links, *links.gather(up_part), (up_part.shape[1],))
    (ffn_down,) = settle(links, *links.gather(down_part), (down_part.shape[1],))
    return inproj, outproj, ffn_up, ffn_down


def small_weights(towers):
    flat = []
    for gain_part, bias_part, upbias_part in towers:
        flat += [gain_part.reshape(-1), bias_part.reshape(-1), upbias_part.reshape(-1)]
    joined = jnp.concatenate(flat)[None]
    whole = lax.all_gather(joined, "wide", axis=0, tiled=True)
    found = []
    at = 0
    for gain_part, bias_part, upbias_part in towers:
        pieces = []
        for part in (gain_part, bias_part):
            taken = whole[:, at : at + part.size].reshape(-1, *part.shape)
            pieces.append(jnp.swapaxes(taken, 0, 1).reshape(part.shape[0], -1))
            at += part.size
        pieces.append(whole[:, at : at + upbias_part.size].reshape(-1))
        at += upbias_part.size
        found.append(pieces)
    return found


def block_order(links, features):
    width = features // links.wide
    column = lax.broadcasted_iota(jnp.int32, (1, features), 1)
    target = links.targets(column // width) * width + column % width
    row = lax.broadcasted_iota(jnp.int32, (features, features), 0)
    chosen = (row == target).astype(jnp.bfloat16)
    return chosen[:, : features // 2], chosen[:, features // 2 :]


def pick(array, chosen):
    return jnp.dot(array, chosen, preferred_element_type=jnp.bfloat16)


def swap_and_add(links, kept, sent):
    return add_low(kept, lax.ppermute(sent, "wide", links.swap))


def term_by_rows(links, orders, left, right):
    kept = contract_rows(pick(left, orders[0]), right)
    sent = contract_rows(pick(left, orders[1]), right).astype(jnp.bfloat16)
    return swap_and_add(links, kept, sent).reshape(links.wide // 2, -1, right.shape[1])


def slot_term(links, left, right):
    tokens, units = left.shape
    block = units // links.wide
    features = right.shape[1]
    half = links.wide // 2
    targets = links.targets(jnp.arange(links.wide, dtype=jnp.int32))
    if block % 128:
        whole = contract_rows(left, right).astype(jnp.bfloat16).reshape(links.wide, block, features)
        ordered = jnp.take(whole, targets, axis=0)
        return swap_and_add(links, ordered[:half], ordered[half:])

    def body(target_ref, left_ref, right_ref, out_ref):
        out_ref[0] = contract_rows(left_ref[...], right_ref[...]).astype(jnp.bfloat16)

    def part(chosen):
        return pl.pallas_call(
            body,
            grid_spec=pltpu.PrefetchScalarGridSpec(
                num_scalar_prefetch=1,
                grid=(half,),
                in_specs=[
                    pl.BlockSpec((tokens, block), lambda k, target: (0, target[k])),
                    pl.BlockSpec((tokens, features), lambda k, target: (0, 0)),
                ],
                out_specs=pl.BlockSpec((1, block, features), lambda k, target: (k, 0, 0)),
            ),
            out_shape=jax.ShapeDtypeStruct((half, block, features), jnp.bfloat16),
            cost_estimate=pl.CostEstimate(
                flops=tokens * units * features,
                bytes_accessed=tokens * units + 2 * tokens * features + units * features,
                transcendentals=0,
            ),
            name="slot_term",
        )(chosen, left, right)

    sent = part(targets[half:])
    return swap_and_add(links, part(targets[:half]), sent)


def tower_pass(links, orders, weights, smalls, buckets):
    inproj, outproj, ffn_up, ffn_down = weights
    gain_rows, biases, up_bias = smalls
    features = inproj.shape[0]
    flat = jnp.concatenate([bucket[0].reshape(-1, features) for bucket in buckets], axis=0)
    joined = matmul(flat, inproj)
    queries = (joined[:, :features] + biases[0]).astype(jnp.bfloat16)
    key_rows = joined[:, features : 2 * features].astype(jnp.bfloat16)
    values = (joined[:, 2 * features :] + biases[1]).astype(jnp.bfloat16)
    blended_parts = []
    logsums = []
    offset = 0
    for bucket in buckets:
        row_count, length = bucket[1].shape
        attended, logsum = attend(
            bucket_rows(queries, offset, row_count, length),
            bucket_rows(key_rows, offset, row_count, length),
            bucket_rows(values, offset, row_count, length),
            bucket[1],
        )
        blended_parts.append(attended.reshape(-1, features))
        logsums.append(logsum)
        offset += row_count * length
    blended = jnp.concatenate(blended_parts, axis=0)
    hidden = flat.astype(jnp.float32) + (matmul(blended, outproj) + biases[2])
    normed_one, scaling_one = normalize(hidden)
    first_out = normed_one * gain_rows[0] + biases[3]
    first_low = first_out.astype(jnp.bfloat16)
    expanded = matmul(first_low, ffn_up) + up_bias
    activated = gelu_exact(expanded).astype(jnp.bfloat16)
    second = first_out + (matmul(activated, ffn_down) + biases[4])
    normed_two, scaling_two = normalize(second)
    result = (normed_two * gain_rows[1] + biases[5]).astype(jnp.bfloat16)
    alive = jnp.concatenate([bucket[1].reshape(-1) for bucket in buckets]).astype(jnp.float32)[
        :, None
    ]
    upstream = (
        jnp.concatenate([bucket[2].reshape(-1, features) for bucket in buckets], axis=0).astype(
            jnp.float32
        )
        * alive
    )
    gain_two = jnp.sum(upstream * normed_two, axis=0)
    shift_two = jnp.sum(upstream, axis=0)
    second_grad = norm_back(upstream, normed_two, scaling_two, gain_rows[1])
    second_low = second_grad.astype(jnp.bfloat16)
    down_bias = jnp.sum(second_low.astype(jnp.float32), axis=0)
    down_sum = links.narrow_sum(links.scatter(slot_term(links, activated, second_low)))
    expanded_grad = (times_transposed(second_low, ffn_down) * gelu_slope(expanded)).astype(
        jnp.bfloat16
    )
    upbias_grad = jnp.sum(expanded_grad.astype(jnp.float32), axis=0)
    up_sum = links.narrow_sum(
        links.scatter(term_by_rows(links, orders, first_low, expanded_grad))
    )
    first_grad = second_grad + times_transposed(expanded_grad, ffn_up)
    gain_one = jnp.sum(first_grad * normed_one, axis=0)
    shift_one = jnp.sum(first_grad, axis=0)
    hidden_grad = norm_back(first_grad, normed_one, scaling_one, gain_rows[0])
    hidden_low = hidden_grad.astype(jnp.bfloat16)
    out_bias = jnp.sum(hidden_low.astype(jnp.float32), axis=0)
    blended_grad = times_transposed(hidden_low, outproj).astype(jnp.bfloat16)
    grad_parts = []
    offset = 0
    for bucket, logsum in zip(buckets, logsums):
        row_count, length = bucket[1].shape
        grad_parts.append(
            attend_back(
                bucket_rows(queries, offset, row_count, length),
                bucket_rows(key_rows, offset, row_count, length),
                bucket_rows(values, offset, row_count, length),
                bucket[1],
                logsum,
                bucket_rows(blended_grad, offset, row_count, length),
            )
        )
        offset += row_count * length
    joined_grad = jnp.concatenate(grad_parts, axis=0)
    input_grad = hidden_grad + times_transposed(joined_grad, inproj)
    query_bias = jnp.sum(joined_grad[:, :features].astype(jnp.float32), axis=0)
    value_bias = jnp.sum(joined_grad[:, 2 * features :].astype(jnp.float32), axis=0)
    bias_grad = jnp.stack([query_bias, value_bias, out_bias, shift_one, down_bias, shift_two])
    gain_grad = jnp.stack([gain_one, gain_two])
    per_row = up_bias.shape[0] // features
    small = jnp.concatenate(
        [gain_grad, bias_grad, upbias_grad.reshape(features, per_row).T], axis=0
    ).astype(jnp.bfloat16)
    small_count = small.shape[0]
    small = jnp.concatenate([small, jnp.zeros((128 - small_count, features), jnp.bfloat16)])

    def front(order):
        return jnp.concatenate(
            [
                contract_rows(pick(flat, order), joined_grad).astype(jnp.bfloat16),
                contract_rows(pick(blended, order), hidden_low).astype(jnp.bfloat16),
                contract_rows(order, small.T).astype(jnp.bfloat16),
            ],
            axis=1,
        )

    front_term = swap_and_add(links, front(orders[0]), front(orders[1]))
    front_term = front_term.reshape(links.wide // 2, -1, front_term.shape[1])
    front_sum = links.narrow_sum(links.scatter(front_term))
    wide_columns = inproj.shape[1]
    small_sum = front_sum[:, wide_columns + features :].T[:small_count]
    reduced = [
        front_sum[:, :wide_columns],
        front_sum[:, wide_columns : wide_columns + features],
        up_sum,
        down_sum,
        small_sum[:2],
        small_sum[2:8],
        small_sum[8:].T.reshape(-1),
    ]
    reduced = [array.astype(jnp.float32) for array in reduced]
    outputs = []
    gradients = []
    offset = 0
    for bucket in buckets:
        row_count, length = bucket[1].shape
        outputs.append(bucket_rows(result, offset, row_count, length))
        gradients.append(bucket_rows(input_grad, offset, row_count, length))
        offset += row_count * length
    return (outputs, gradients, tuple(reduced))


def per_device(
    links,
    query_tokens,
    query_mask,
    short_tokens,
    short_mask,
    long_tokens,
    long_mask,
    long_count,
    query_inproj,
    query_outproj,
    query_ffn_up,
    query_ffn_down,
    query_gains,
    query_biases,
    query_up_bias,
    passage_inproj,
    passage_outproj,
    passage_ffn_up,
    passage_ffn_down,
    passage_gains,
    passage_biases,
    passage_up_bias,
    query_upstream,
    short_upstream,
    long_upstream,
):
    long_slots = long_mask.shape[0]
    slot_alive = (jnp.arange(long_slots, dtype=jnp.int32) < long_count[0]).astype(jnp.int32)
    alive_long = long_mask * slot_alive[:, None]
    query_small, passage_small = small_weights(
        (
            (query_gains, query_biases, query_up_bias),
            (passage_gains, passage_biases, passage_up_bias),
        )
    )
    orders = block_order(links, query_tokens.shape[-1])
    passage_weights = fetch(
        links, (passage_inproj, passage_outproj, passage_ffn_up, passage_ffn_down)
    )
    query_weights = fetch(links, (query_inproj, query_outproj, query_ffn_up, query_ffn_down))
    passage_results, passage_inputs, passage_grads = tower_pass(
        links,
        orders,
        passage_weights,
        passage_small,
        [(short_tokens, short_mask, short_upstream), (long_tokens, alive_long, long_upstream)],
    )
    query_results, query_inputs, query_grads = tower_pass(
        links,
        orders,
        query_weights,
        query_small,
        [(query_tokens, query_mask, query_upstream)],
    )
    return (
        (
            query_results[0],
            passage_results[0],
            passage_results[1],
            query_inputs[0],
            passage_inputs[0],
            passage_inputs[1],
        )
        + query_grads
        + passage_grads
    )


def solution(mesh):
    in_specs = (
        P(("wide", "narrow"), None, None),
        P(("wide", "narrow"), None),
        P(("wide", "narrow"), None, None),
        P(("wide", "narrow"), None),
        P(("wide", "narrow"), None, None),
        P(("wide", "narrow"), None),
        P(("wide", "narrow")),
        P("wide", None),
        P("wide", None),
        P("wide", None),
        P("wide", None),
        P(None, "wide"),
        P(None, "wide"),
        P("wide"),
        P("wide", None),
        P("wide", None),
        P("wide", None),
        P("wide", None),
        P(None, "wide"),
        P(None, "wide"),
        P("wide"),
        P(("wide", "narrow"), None, None),
        P(("wide", "narrow"), None, None),
        P(("wide", "narrow"), None, None),
    )
    out_specs = (
        P(("wide", "narrow"), None, None),
        P(("wide", "narrow"), None, None),
        P(("wide", "narrow"), None, None),
        P(("wide", "narrow"), None, None),
        P(("wide", "narrow"), None, None),
        P(("wide", "narrow"), None, None),
        P("wide", None),
        P("wide", None),
        P("wide", None),
        P("wide", None),
        P(None, "wide"),
        P(None, "wide"),
        P("wide"),
        P("wide", None),
        P("wide", None),
        P("wide", None),
        P("wide", None),
        P(None, "wide"),
        P(None, "wide"),
        P("wide"),
    )
    return jax.shard_map(
        functools.partial(per_device, Links(mesh)), mesh=mesh, in_specs=in_specs, out_specs=out_specs, check_vma=False
    )
```

```python
import functools

import jax
import jax.numpy as jnp
import numpy as np
from jax import lax
from jax.experimental import pallas as pl
from jax.experimental.pallas import tpu as pltpu
from jax.sharding import PartitionSpec as P

HEADS = 12


EPSILON = 1e-05
NEGATIVE = -1000000000.0
OUTSIDE = -2e38
ROOT_HALF = 0.7071067811865476
INV_ROOT_TAU = 0.3989422804014327
LANES = 128
SMALL_ROWS = 8
VMEM_BYTES = 60 * 1024 * 1024


def matmul(left, right):
    return jnp.dot(left, right, preferred_element_type=jnp.float32)


def contract_rows(left, right):
    return lax.dot_general(
        left, right, (((0,), (0,)), ((), ())), preferred_element_type=jnp.float32
    )


def times_transposed(left, right):
    return lax.dot_general(
        left, right, (((1,), (1,)), ((), ())), preferred_element_type=jnp.float32
    )


def normalize(hidden):
    center = hidden - jnp.mean(hidden, axis=-1, keepdims=True)
    scaling = lax.rsqrt(jnp.mean(center * center, axis=-1, keepdims=True) + EPSILON)
    return (center * scaling, scaling)


def norm_back(upstream, normed, scaling, gain):
    scaled = upstream * gain
    return scaling * (
        scaled
        - jnp.mean(scaled, axis=-1, keepdims=True)
        - normed * jnp.mean(scaled * normed, axis=-1, keepdims=True)
    )


def gelu_exact(values):
    return 0.5 * values * (1.0 + lax.erf(values * ROOT_HALF))


def gelu_slope(values):
    return (
        0.5 * (1.0 + lax.erf(values * ROOT_HALF))
        + values * jnp.exp(-0.5 * values * values) * INV_ROOT_TAU
    )


def add_low(left, right):
    return (left.astype(jnp.float32) + right.astype(jnp.float32)).astype(jnp.bfloat16)


def tie(*arrays):
    return lax.optimization_barrier(arrays)


def probabilities(queries, keys, visible, rows, length):
    scores = times_transposed(queries, keys) * queries.shape[-1] ** (-0.5)
    scores = jnp.where(visible > 0, scores, NEGATIVE)
    if rows != length:
        row = lax.broadcasted_iota(jnp.int32, (rows, rows), 0) // length
        column = lax.broadcasted_iota(jnp.int32, (rows, rows), 1) // length
        scores = jnp.where(row == column, scores, OUTSIDE)
    exponent = jnp.exp(scores - jnp.max(scores, axis=-1, keepdims=True))
    return exponent / jnp.sum(exponent, axis=-1, keepdims=True)


def attention_cost(qkv, spans, scale):
    work = sum(rows * rows for _, rows, _ in spans)
    return pl.CostEstimate(
        flops=4 * scale * work * qkv.shape[1] // 3,
        bytes_accessed=scale * 3 * qkv.size,
        transcendentals=HEADS * work,
    )


def attend(qkv, alive_row, spans):
    tokens, features = qkv.shape[0], qkv.shape[1] // 3
    head = features // HEADS
    pair = 2 * head

    def body(qkv_ref, alive_ref, out_ref):
        @pl.loop(0, HEADS // 2)
        def _(at):
            base = pl.multiple_of(at * pair, pair)
            for start, rows, length in spans:
                inside = pl.ds(start, rows)
                queries, keys, values = (
                    qkv_ref[inside, pl.ds(pl.multiple_of(base + part * features, pair), pair)]
                    for part in range(3)
                )
                visible = alive_ref[:, start : start + rows]
                found = []
                for lane in (0, head):
                    cut = slice(lane, lane + head)
                    probs = probabilities(queries[:, cut], keys[:, cut], visible, rows, length)
                    found.append(matmul(probs.astype(jnp.bfloat16), values[:, cut]))
                out_ref[inside, pl.ds(base, pair)] = jnp.concatenate(found, axis=1).astype(
                    jnp.bfloat16
                )

    return pl.pallas_call(
        body,
        out_shape=jax.ShapeDtypeStruct((tokens, features), jnp.bfloat16),
        cost_estimate=attention_cost(qkv, spans, 1),
        name="attend",
    )(qkv, alive_row)


def attend_back(qkv, alive_row, upstream, spans):
    tokens, features = upstream.shape
    head = features // HEADS
    pair = 2 * head
    factor = head ** (-0.5)

    def body(qkv_ref, alive_ref, upstream_ref, out_ref, sum_ref):
        @pl.loop(0, HEADS // 2)
        def _(at):
            base = pl.multiple_of(at * pair, pair)
            places = [pl.ds(pl.multiple_of(base + part * features, pair), pair) for part in range(3)]
            totals = [jnp.zeros((1, pair), jnp.float32) for _ in range(3)]
            for start, rows, length in spans:
                inside = pl.ds(start, rows)
                queries, keys, values = (qkv_ref[inside, place] for place in places)
                above = upstream_ref[inside, pl.ds(base, pair)]
                visible = alive_ref[:, start : start + rows]
                found = ([], [], [])
                for lane in (0, head):
                    cut = slice(lane, lane + head)
                    query, key, value, up = queries[:, cut], keys[:, cut], values[:, cut], above[:, cut]
                    probs = probabilities(query, key, visible, rows, length)
                    found[2].append(contract_rows(probs.astype(jnp.bfloat16), up))
                    prob_grad = times_transposed(up, value)
                    crossing = jnp.sum(probs * prob_grad, axis=-1, keepdims=True)
                    score_grad = (probs * (prob_grad - crossing)).astype(jnp.bfloat16)
                    found[0].append(matmul(score_grad, key) * factor)
                    found[1].append(contract_rows(score_grad, query) * factor)
                for part, pieces in enumerate(found):
                    both = jnp.concatenate(pieces, axis=1).astype(jnp.bfloat16)
                    out_ref[inside, places[part]] = both
                    totals[part] += jnp.sum(both.astype(jnp.float32), axis=0, keepdims=True)
            for part, total in enumerate(totals):
                sum_ref[:, places[part]] = total

    return pl.pallas_call(
        body,
        out_shape=(
            jax.ShapeDtypeStruct(qkv.shape, jnp.bfloat16),
            jax.ShapeDtypeStruct((1, qkv.shape[1]), jnp.float32),
        ),
        cost_estimate=attention_cost(qkv, spans, 3),
        name="attend_back",
    )(qkv, alive_row, upstream)


class Links:
    def __init__(self, mesh):
        self.wide = mesh.shape["wide"]
        self.narrow = mesh.shape["narrow"]
        levels = self.wide.bit_length() - 1
        upward = list(range(1, levels))
        self.orders = (upward, upward[1:] + upward[:1])
        self.steps = [
            [(w, w ^ (1 << self.orders[w & 1][s])) for w in range(self.wide)]
            for s in range(levels - 1)
        ]
        self.swap = [(w, w ^ 1) for w in range(self.wide)]

    def mask(self, slot, core):
        return sum(((slot >> s) & 1) << bit for s, bit in enumerate(self.orders[core]))

    def slot_masks(self, core):
        half = self.wide // 2
        return [self.mask(k, core) for k in range(half)] + [
            1 ^ self.mask(k, 1 - core) for k in range(half)
        ]

    def slot_target(self, spot, slot):
        first, second = (self.slot_masks(core)[slot] for core in (0, 1))
        return spot ^ jnp.where((spot & 1) == 0, first, second)

    def all_targets(self):
        spot = lax.axis_index("wide").astype(jnp.int32)
        tables = [np.array(self.slot_masks(core), np.int32) for core in (0, 1)]
        return spot ^ jnp.where((spot & 1) == 0, tables[0], tables[1])

    def swapped(self, array):
        return lax.ppermute(array, "wide", self.swap)


class Gather:
    def __init__(self, links, packed):
        self.links = links
        self.held = packed[None]
        self.step = 0
        self.got = None

    def send(self, *after):
        if after:
            self.held = tie(self.held, *after)[0]
        self.got = lax.ppermute(self.held, "wide", self.links.steps[self.step])
        self.step += 1
        return self.got

    def merge(self):
        self.held = jnp.concatenate([self.held, self.got], axis=0)

    def run(self):
        while self.step < len(self.links.steps):
            if self.step:
                self.merge()
            self.send()

    def pieces(self):
        own = (self.held, self.got)
        return own + tuple(self.links.swapped(piece) for piece in own)


def settle(links, pieces, layout):
    quarter, rows, columns = pieces[0].shape
    count = links.wide
    shapes = [(count, rows * stacked, width) for _, width, stacked in layout]
    if rows % 16:
        slots = jnp.concatenate(pieces, axis=0)
        source = links.all_targets()
        ordered = jnp.take(slots, jnp.argsort(source), axis=0)
        outs = []
        for column, width, stacked in layout:
            cut = ordered[:, :, column : column + width * stacked]
            cut = cut.reshape(count, rows, stacked, width)
            outs.append(jnp.swapaxes(cut, 1, 2).reshape(-1, width))
        return outs
    moves = [
        (out, i, column + i * width, width)
        for out, (column, width, stacked) in enumerate(layout)
        for i in range(stacked)
    ]

    def body(*refs):
        sources, outs = refs[:4], refs[4 : 4 + len(layout)]
        buffer, in_sem, out_sem = refs[4 + len(layout) :]
        spot = lax.axis_index("wide").astype(jnp.int32)
        arriving = []
        for slot in range(count):
            copy = pltpu.make_async_copy(
                sources[slot // quarter].at[slot % quarter], buffer.at[slot], in_sem.at[slot]
            )
            copy.start()
            arriving.append(copy)
        leaving = []
        for slot in range(count):
            arriving[slot].wait()
            target = links.slot_target(spot, slot)
            for at, (out, i, column, width) in enumerate(moves):
                copy = pltpu.make_async_copy(
                    buffer.at[slot, :, pl.ds(column, width)],
                    outs[out].at[target, pl.ds(i * rows, rows), :],
                    out_sem.at[slot, at],
                )
                copy.start()
                leaving.append(copy)
        for copy in leaving:
            copy.wait()

    outs = pl.pallas_call(
        body,
        in_specs=[pl.BlockSpec(memory_space=pl.ANY)] * 4,
        out_specs=[pl.BlockSpec(memory_space=pl.ANY)] * len(layout),
        out_shape=[jax.ShapeDtypeStruct(shape, jnp.bfloat16) for shape in shapes],
        scratch_shapes=[
            pltpu.VMEM((count, rows, columns), jnp.bfloat16),
            pltpu.SemaphoreType.DMA((count,)),
            pltpu.SemaphoreType.DMA((count, len(moves))),
        ],
        cost_estimate=pl.CostEstimate(
            flops=0, bytes_accessed=4 * count * rows * columns, transcendentals=0
        ),
        name="settle",
    )(*pieces)
    return [out.reshape(-1, out.shape[-1]) for out in outs]


def pack_tower(parts):
    inproj_part, outproj_part, up_part, down_part = parts
    rows = inproj_part.shape[0]
    stacked = down_part.shape[0] // rows
    front = [inproj_part, outproj_part]
    back = [up_part] + [down_part[i * rows : (i + 1) * rows] for i in range(stacked)]
    return front, back, stacked


def front_layout(features):
    return [(0, 3 * features, 1), (3 * features, features, 1)]


def back_layout(features, units, stacked, start=0):
    return [(start, units, 1), (start + units, features, stacked)]


def small_weights(links, order, towers):
    rows = towers[0][0].shape[1]
    units = towers[0][2].shape[0]
    if rows % 16 or units % LANES or rows > LANES:
        found = []
        for gain_part, bias_part, upbias_part in towers:
            both = jnp.concatenate([gain_part, bias_part])
            found.append(
                (
                    lax.all_gather(both, "wide", axis=1, tiled=True),
                    lax.all_gather(upbias_part, "wide", axis=0, tiled=True),
                )
            )
        return found
    pad_rows = units // LANES
    each = -(-(SMALL_ROWS + pad_rows) // 8) * 8
    lines = []
    for gain_part, bias_part, upbias_part in towers:
        lines.append(jnp.pad(gain_part, ((0, 0), (0, LANES - rows))))
        lines.append(jnp.pad(bias_part, ((0, 0), (0, LANES - rows))))
        lines.append(upbias_part.reshape(pad_rows, LANES))
        lines.append(jnp.zeros((each - SMALL_ROWS - pad_rows, LANES), jnp.float32))
    gather = Gather(links, jnp.concatenate(lines))
    gather.run()
    pieces = gather.pieces()
    quarter = pieces[0].shape[0]
    count = links.wide
    features = rows * count

    def body(*refs):
        sources, order_ref, main_ref, up_ref = refs[:4], refs[4], refs[5], refs[6]
        spot = lax.axis_index("wide").astype(jnp.int32)
        blocks = []
        for slot in range(count):
            block = sources[slot // quarter][slot % quarter]
            target = links.slot_target(spot, slot)
            for tower in range(len(towers)):
                first = tower * each + SMALL_ROWS
                up_ref[target, tower] = block[first : first + pad_rows]
            blocks.append(block[:, :rows])
        slots = jnp.concatenate(blocks, axis=1)
        main_ref[...] = lax.dot_general(
            slots,
            order_ref[...].astype(jnp.float32),
            (((1,), (1,)), ((), ())),
            precision=lax.Precision.HIGHEST,
            preferred_element_type=jnp.float32,
        )

    main, up = pl.pallas_call(
        body,
        out_shape=(
            jax.ShapeDtypeStruct((each * len(towers), features), jnp.float32),
            jax.ShapeDtypeStruct((count, len(towers), pad_rows, LANES), jnp.float32),
        ),
        name="settle_small",
    )(*pieces, order)
    return [
        (main[t * each : t * each + SMALL_ROWS], up[:, t].reshape(-1)) for t in range(len(towers))
    ]


def block_order(links, features):
    width = features // links.wide

    def fill(out_ref):
        spot = lax.axis_index("wide").astype(jnp.int32)
        column = lax.broadcasted_iota(jnp.int32, (1, features), 1)
        target = jnp.zeros_like(column)
        for slot in range(links.wide):
            inside = (column >= slot * width) & (column < (slot + 1) * width)
            first = links.slot_target(spot, slot) * width - slot * width
            target = jnp.where(inside, column + first, target)
        row = lax.broadcasted_iota(jnp.int32, (features, features), 0)
        out_ref[...] = jnp.where(row == target, 1.0, 0.0).astype(jnp.bfloat16)

    return pl.pallas_call(
        fill,
        out_shape=jax.ShapeDtypeStruct((features, features), jnp.bfloat16),
        name="block_order",
    )()


def pick(array, chosen):
    return jnp.dot(array, chosen, preferred_element_type=jnp.bfloat16)


def halves_by_rows(links, left, right):
    half = left.shape[1] // 2
    sent = contract_rows(left[:, half:], right).astype(jnp.bfloat16)
    kept = contract_rows(left[:, :half], right).astype(jnp.bfloat16)
    shape = (links.wide // 2, -1, right.shape[1])
    return kept.reshape(shape), sent.reshape(shape)


def halves_of_units(links, left, right, stacked):
    tokens, units = left.shape
    block = units // links.wide
    rows = block // stacked
    features = right.shape[1]
    half = links.wide // 2
    if block % LANES or rows % 16:
        whole = contract_rows(left, right).astype(jnp.bfloat16)
        whole = jnp.take(
            whole.reshape(links.wide, stacked, rows, features), links.all_targets(), axis=0
        )
        whole = jnp.swapaxes(whole, 1, 2).reshape(links.wide, rows, stacked * features)
        return whole[:half], whole[half:]

    def part(first, name):
        def body(left_ref, right_ref, out_ref):
            spot = lax.axis_index("wide").astype(jnp.int32)
            for k in range(half):
                target = links.slot_target(spot, first + k)
                found = contract_rows(
                    left_ref[:, pl.ds(pl.multiple_of(target * block, LANES), block)], right_ref[...]
                ).astype(jnp.bfloat16)
                for i in range(stacked):
                    out_ref[k, :, i * features : (i + 1) * features] = found[
                        i * rows : (i + 1) * rows
                    ]

        return pl.pallas_call(
            body,
            out_shape=jax.ShapeDtypeStruct((half, rows, stacked * features), jnp.bfloat16),
            cost_estimate=pl.CostEstimate(
                flops=tokens * units * features,
                bytes_accessed=2 * tokens * (units + features) + units * features,
                transcendentals=0,
            ),
            name=name,
        )(left, right)

    sent = part(half, "units_sent")
    return part(0, "units_kept"), sent


class Scatter:
    def __init__(self, links, terms):
        self.links = links
        self.terms = terms
        self.left = list(links.steps)
        self.got = None

    def send(self):
        half = self.terms.shape[0] // 2
        self.got = lax.ppermute(self.terms[half:], "wide", self.left.pop())
        return self.got

    def land(self):
        self.terms = add_low(self.terms[: self.terms.shape[0] // 2], self.got)
        self.got = None
        return self.terms

    def run(self):
        if self.got is not None:
            self.land()
        while self.left:
            self.send()
            self.land()
        return self.terms[0]


class NarrowSum:
    def __init__(self, links, terms):
        self.count = links.narrow
        self.terms = terms
        self.native = bool(self.count & (self.count - 1)) or terms.shape[0] % self.count != 0
        self.plan = []
        stride = 1
        while stride < self.count:
            self.plan.append((True, stride))
            stride *= 2
        self.plan += [(False, stride) for _, stride in reversed(self.plan)]
        if self.native:
            self.plan = [None]

    def step(self):
        if self.native:
            self.terms = lax.psum(self.terms, "narrow")
            self.plan = []
            return self.terms
        adding, stride = self.plan.pop(0)
        swap = [(z, z ^ stride) for z in range(self.count)]
        low_side = (lax.axis_index("narrow") & stride) == 0
        terms = self.terms
        if adding:
            half = terms.shape[0] // 2
            kept = jnp.where(low_side, terms[:half], terms[half:])
            sent = jnp.where(low_side, terms[half:], terms[:half])
            got = lax.ppermute(sent, "narrow", swap)
            self.terms = lax.optimization_barrier(add_low(kept, got))
        else:
            got = lax.ppermute(terms, "narrow", swap)
            self.terms = jnp.where(
                low_side,
                jnp.concatenate([terms, got], axis=0),
                jnp.concatenate([got, terms], axis=0),
            )
        return self.terms

    def run(self):
        while self.plan:
            self.step()
        return self.terms


class Tower:
    def __init__(self, links, order, smalls, buckets):
        main, self.up_bias = smalls
        self.links, self.order = links, order
        self.gains, self.biases = main[:2], main[2:8]
        self.buckets = buckets
        self.features = main.shape[1]
        self.spans = []
        offset = 0
        for tokens, _, _, grouped in buckets:
            count, length = tokens.shape[:2]
            rows = count * length if grouped else length
            self.spans += [
                (offset + start, rows, length) for start in range(0, count * length, rows)
            ]
            offset += count * length
        self.flat = jnp.concatenate([b[0].reshape(-1, self.features) for b in buckets])
        alive = jnp.concatenate([b[1].reshape(-1) for b in buckets]).astype(jnp.float32)
        self.alive_row = alive[None]
        self.upstream = (
            jnp.concatenate([b[2].reshape(-1, self.features) for b in buckets]).astype(jnp.float32)
            * alive[:, None]
        )

    def project(self, inproj):
        zeros = jnp.zeros((self.features,), jnp.float32)
        bias = jnp.concatenate([self.biases[0], zeros, self.biases[1]])
        self.inproj = inproj
        self.qkv = (matmul(self.flat, inproj) + bias).astype(jnp.bfloat16)

    def attend(self):
        self.blended = attend(self.qkv, self.alive_row, self.spans)

    def join(self, outproj):
        self.outproj = outproj
        hidden = self.flat.astype(jnp.float32) + (matmul(self.blended, outproj) + self.biases[2])
        self.normed_one, self.scaling_one = normalize(hidden)
        self.first_out = self.normed_one * self.gains[0] + self.biases[3]
        self.first_low = self.first_out.astype(jnp.bfloat16)

    def expand(self, ffn_up):
        self.ffn_up = ffn_up
        self.expanded = matmul(self.first_low, ffn_up) + self.up_bias
        self.activated = gelu_exact(self.expanded).astype(jnp.bfloat16)

    def contract(self, ffn_down):
        self.ffn_down = ffn_down
        second = self.first_out + (matmul(self.activated, ffn_down) + self.biases[4])
        normed, scaling = normalize(second)
        self.result = (normed * self.gains[1] + self.biases[5]).astype(jnp.bfloat16)
        self.gain_two = jnp.sum(self.upstream * normed, axis=0)
        self.shift_two = jnp.sum(self.upstream, axis=0)
        self.second_grad = norm_back(self.upstream, normed, scaling, self.gains[1])
        self.second_low = self.second_grad.astype(jnp.bfloat16)
        self.down_bias = jnp.sum(self.second_low.astype(jnp.float32), axis=0)

    def down_halves(self):
        stacked = self.ffn_down.shape[0] // self.features
        return halves_of_units(self.links, self.activated, self.second_low, stacked)

    def expand_back(self):
        self.expanded_grad = (
            times_transposed(self.second_low, self.ffn_down) * gelu_slope(self.expanded)
        ).astype(jnp.bfloat16)
        self.upbias_grad = jnp.sum(self.expanded_grad.astype(jnp.float32), axis=0)

    def up_halves(self):
        return halves_by_rows(self.links, pick(self.first_low, self.order), self.expanded_grad)

    def join_back(self):
        first_grad = self.second_grad + times_transposed(self.expanded_grad, self.ffn_up)
        self.gain_one = jnp.sum(first_grad * self.normed_one, axis=0)
        self.shift_one = jnp.sum(first_grad, axis=0)
        self.hidden_grad = norm_back(
            first_grad, self.normed_one, self.scaling_one, self.gains[0]
        )
        self.hidden_low = self.hidden_grad.astype(jnp.bfloat16)
        self.out_bias = jnp.sum(self.hidden_low.astype(jnp.float32), axis=0)
        self.blended_grad = times_transposed(self.hidden_low, self.outproj).astype(jnp.bfloat16)

    def outproj_halves(self):
        return halves_by_rows(self.links, pick(self.blended, self.order), self.hidden_low)

    def attend_back(self):
        self.joined_grad, sums = attend_back(
            self.qkv, self.alive_row, self.blended_grad, self.spans
        )
        features = self.features
        self.query_bias, self.value_bias = sums[0, :features], sums[0, 2 * features :]

    def front_halves(self):
        kept, sent = halves_by_rows(self.links, pick(self.flat, self.order), self.joined_grad)
        per_row = self.up_bias.shape[0] // self.features
        small = jnp.stack(
            [
                self.gain_one,
                self.gain_two,
                self.query_bias,
                self.value_bias,
                self.out_bias,
                self.shift_one,
                self.down_bias,
                self.shift_two,
            ]
        )
        units = self.upbias_grad.reshape(self.features, per_row).T
        small = jnp.concatenate([small, units]).astype(jnp.bfloat16)
        small = jnp.pad(small, ((0, LANES - small.shape[0]), (0, 0)))
        columns = contract_rows(self.order, small.T).astype(jnp.bfloat16)
        columns = columns.reshape(self.links.wide, -1, LANES)
        half = self.links.wide // 2
        return (
            jnp.concatenate([kept, columns[:half]], axis=2),
            jnp.concatenate([sent, columns[half:]], axis=2),
        )

    def input_back(self):
        input_grad = self.hidden_grad + times_transposed(self.joined_grad, self.inproj)
        offset = 0
        self.outputs, self.input_grads = [], []
        for tokens, _, _, _ in self.buckets:
            count = tokens.shape[0] * tokens.shape[1]
            self.outputs.append(self.result[offset : offset + count].reshape(tokens.shape))
            self.input_grads.append(input_grad[offset : offset + count].reshape(tokens.shape))
            offset += count

    def gradients(self, back, front):
        features, units = self.features, self.up_bias.shape[0]
        stacked = units // features
        back, front = back.astype(jnp.float32), front.astype(jnp.float32)
        down = back[:, units : units + stacked * features]
        down = jnp.concatenate([down[:, i * features : (i + 1) * features] for i in range(stacked)])
        small = front[:, 3 * features :]
        return (
            front[:, : 3 * features],
            back[:, units + stacked * features :],
            back[:, :units],
            down,
            small[:, :2].T,
            small[:, 2:8].T,
            small[:, 8 : 8 + stacked].reshape(-1),
        )


def chunk(links, *halves):
    return jnp.concatenate([add_low(kept, links.swapped(sent)) for kept, sent in halves], axis=2)


def per_device(
    links,
    query_tokens,
    query_mask,
    short_tokens,
    short_mask,
    long_tokens,
    long_mask,
    long_count,
    query_inproj,
    query_outproj,
    query_ffn_up,
    query_ffn_down,
    query_gains,
    query_biases,
    query_up_bias,
    passage_inproj,
    passage_outproj,
    passage_ffn_up,
    passage_ffn_down,
    passage_gains,
    passage_biases,
    passage_up_bias,
    query_upstream,
    short_upstream,
    long_upstream,
):
    features = query_tokens.shape[-1]
    units = query_up_bias.shape[0] * links.wide
    long_slots = long_mask.shape[0]
    slot_alive = (jnp.arange(long_slots, dtype=jnp.int32) < long_count[0]).astype(jnp.int32)
    alive_long = long_mask * slot_alive[:, None]

    front, back, stacked = pack_tower(
        (passage_inproj, passage_outproj, passage_ffn_up, passage_ffn_down)
    )
    front_query, back_query, _ = pack_tower(
        (query_inproj, query_outproj, query_ffn_up, query_ffn_down)
    )
    first = Gather(links, jnp.concatenate(front, axis=1))
    second = Gather(links, jnp.concatenate(back, axis=1))
    third = Gather(links, jnp.concatenate(front_query + back_query, axis=1))

    landed = first.send()
    order = block_order(links, features)
    query_small, passage_small = small_weights(
        links,
        order,
        (
            (query_gains, query_biases, query_up_bias),
            (passage_gains, passage_biases, passage_up_bias),
        ),
    )
    second.send(landed)
    first.run()
    inproj, outproj = settle(links, first.pieces(), front_layout(features))
    passage = Tower(
        links,
        order,
        passage_small,
        [
            (long_tokens, alive_long, long_upstream, False),
            (short_tokens, short_mask, short_upstream, False),
        ],
    )
    query = Tower(links, order, query_small, [(query_tokens, query_mask, query_upstream, True)])
    passage.project(inproj)
    passage.qkv, second.got = tie(passage.qkv, second.got)
    second.run()
    passage.attend()
    passage.join(outproj)
    third.send(second.got)
    ffn_up, ffn_down = settle(links, second.pieces(), back_layout(features, units, stacked))
    passage.expand(ffn_up)
    passage.contract(ffn_down)
    passage.second_low, third.got = tie(passage.second_low, third.got)
    third.run()
    down = passage.down_halves()
    passage.expand_back()
    up = passage.up_halves()
    passage.join_back()
    out = passage.outproj_halves()
    passage_back = Scatter(links, chunk(links, up, down, out))
    passage_back.send()
    passage.blended_grad, third.got, passage_back.terms = tie(
        passage.blended_grad, third.got, passage_back.terms
    )
    pieces = third.pieces()
    passage.attend_back()
    front_halves = passage.front_halves()
    passage.input_back()

    weights = settle(
        links, pieces, front_layout(features) + back_layout(features, units, stacked, 4 * features)
    )
    passage_front = Scatter(links, chunk(links, front_halves))
    passage_back.got, weights[0], passage_front.terms = tie(
        passage_back.got, weights[0], passage_front.terms
    )
    passage_back.land()
    if passage_back.left:
        passage_back.send()
    passage_front.send()
    query.project(weights[0])
    query.attend()
    query.blended, passage_front.got, passage_back.got = tie(
        query.blended, passage_front.got, passage_back.got
    )
    passage_back.land()
    passage_front.land()
    passage_total = jnp.concatenate([passage_back.run(), passage_front.run()], axis=1)
    query.join(weights[1])
    query.first_low, passage_total = tie(query.first_low, passage_total)
    passage_sum = NarrowSum(links, passage_total)
    query.expand(weights[2])
    query.contract(weights[3])
    passage_sum.step()
    query.second_low, passage_sum.terms = tie(query.second_low, passage_sum.terms)
    down = query.down_halves()
    query.expand_back()
    up = query.up_halves()
    if passage_sum.plan:
        passage_sum.step()
    query.expanded_grad, passage_sum.terms = tie(query.expanded_grad, passage_sum.terms)
    query.join_back()
    out = query.outproj_halves()
    query_back = Scatter(links, chunk(links, up, down, out))
    query_back.send()
    query.blended_grad, query_back.terms = tie(query.blended_grad, query_back.terms)
    query.attend_back()
    query_front = Scatter(links, chunk(links, query.front_halves()))
    query.input_back()
    query_front_sum = NarrowSum(links, query_front.run())
    query_back_sum = NarrowSum(links, query_back.run())
    passage_total = passage_sum.run()
    split = units + (stacked + 1) * features
    return (
        query.outputs[0],
        passage.outputs[1],
        passage.outputs[0],
        query.input_grads[0],
        passage.input_grads[1],
        passage.input_grads[0],
        *query.gradients(query_back_sum.run(), query_front_sum.run()),
        *passage.gradients(passage_total[:, :split], passage_total[:, split:]),
    )


def solution(mesh):
    in_specs = (
        P(("wide", "narrow"), None, None),
        P(("wide", "narrow"), None),
        P(("wide", "narrow"), None, None),
        P(("wide", "narrow"), None),
        P(("wide", "narrow"), None, None),
        P(("wide", "narrow"), None),
        P(("wide", "narrow")),
        P("wide", None),
        P("wide", None),
        P("wide", None),
        P("wide", None),
        P(None, "wide"),
        P(None, "wide"),
        P("wide"),
        P("wide", None),
        P("wide", None),
        P("wide", None),
        P("wide", None),
        P(None, "wide"),
        P(None, "wide"),
        P("wide"),
        P(("wide", "narrow"), None, None),
        P(("wide", "narrow"), None, None),
        P(("wide", "narrow"), None, None),
    )
    out_specs = (
        P(("wide", "narrow"), None, None),
        P(("wide", "narrow"), None, None),
        P(("wide", "narrow"), None, None),
        P(("wide", "narrow"), None, None),
        P(("wide", "narrow"), None, None),
        P(("wide", "narrow"), None, None),
        P("wide", None),
        P("wide", None),
        P("wide", None),
        P("wide", None),
        P(None, "wide"),
        P(None, "wide"),
        P("wide"),
        P("wide", None),
        P("wide", None),
        P("wide", None),
        P("wide", None),
        P(None, "wide"),
        P(None, "wide"),
        P("wide"),
    )
    return jax.shard_map(
        functools.partial(per_device, Links(mesh)), mesh=mesh, in_specs=in_specs, out_specs=out_specs, check_vma=False
    )
```
